768 devices in a mesh: slab: 192 (over z, y_hi, x, core), dom: 4 (over y_lo).
Axes of the slice: x: 4, y: 8 (y_hi: 2, y_lo: 4; y = y_hi * 4 + y_lo), z: 12, core: 2. Of those that a mesh axis runs over, the one named last changes fastest.
Arguments:
- positions: float32 [3, 4718592], P(None, ('slab', 'dom')), may hold values from -6 to 6
- velocities: float32 [3, 4718592], P(None, ('slab', 'dom')), may hold values from -6 to 6
- masses: float32 [4718592], P(('slab', 'dom')), may hold values from 0.2 to 2
- owner_cell: int32 [4718592, 1], P(('slab', 'dom')), may hold values from 0 to 255; in each aligned block of 6144 rows (0 to 6143, 6144 to 12287, ...) at most 32 rows name the same one
- counts: int32 [768], P(('slab', 'dom')), may hold values from 3072 to 6144, as said below
Outputs:
- state: float32 [10, 192, 256, 128], P(None, 'slab', 'dom')
- buddy: float32 [10, 192, 256, 128], P(None, 'slab', 'dom')
The draws below stay inside these ranges and needn't reach their ends.
Inputs may be any that keep to these rules, and one draw needn't show every extreme that they name: owner_cell is the partner index of the owner times 64 plus its cell; among the rows of one device no value appears more than 32 times, and some device's rows name one value exactly 32 times. `counts`: some device has all 6144 rows live.
All inputs are finite; a program needn't handle non-finite values.
Results may differ from the reference program's by a relative error of at most 0.0003.
Values sent between devices are 32-bit elements; how exact they have to be, the bound alone decides.
A program may use at most 32 MiB of HBM per device.

```python
import math
import jax
import jax.numpy as jnp
import numpy as np
from jax import lax

CELLS = 64
TILE = 128
PART_DEV = 6144
SLOT = 32
NCELL = 256
GROUPS = 768
PARTICLES = 4718592
N_SLAB = 192
N_DOM = 4


def draw_counts(key, part):
    values = jax.random.randint(key, (GROUPS,), PART_DEV // 2, PART_DEV + 1)
    chosen = jax.random.randint(jax.random.fold_in(key, 7), (), 0, GROUPS)
    return jnp.where(jnp.arange(GROUPS) == chosen, PART_DEV, values).astype(jnp.int32)


def block_scale(key, extent, shards, low, largest):
    loudness = 1.0
    for dim, shards_of in shards:
        draws = jax.random.uniform(jax.random.fold_in(jax.random.fold_in(key, 6), dim), (shards_of,), jnp.float32, low / len(shards), largest / len(shards))
        loudness = loudness * jnp.repeat(jnp.exp(draws), extent[dim] // shards_of).reshape((-1,) + (1,) * (len(extent) - 1 - dim))
    return loudness


def routed_block(own_key, own, number, rows, count, top, bound, lean):
    sequence = jax.random.permutation(own_key, count)
    heavy_load, usual = shares(count, rows * top, bound, lean, True), shares(count, rows * top, bound, lean, False)
    places = jnp.arange(count)

    def named(sizes, turn):
        used = int((sizes > 0).sum())
        fixed = max(1, used // 4)
        shifted = fixed + (places - fixed + turn * (used - fixed)) % max(1, count - fixed)
        return jnp.zeros((count,), jnp.int32).at[sequence[jnp.where(places < fixed, places, shifted)]].set(jnp.asarray(sizes, jnp.int32))

    sizes = jnp.where(number % 4 == 0, named(heavy_load, number // 4), named(usual, number - number // 4 - 1))
    mixed = jax.random.permutation(jax.random.fold_in(own, 3), count)
    donor, taker = mixed[0:count // 2 * 2:2], mixed[1:count // 2 * 2:2]
    margin = jnp.minimum(sizes[donor] - 1, bound - sizes[taker]) // 2
    margin = jnp.where((donor == sequence[0]) | (taker == sequence[0]) | (sizes[taker] == 0), 0, jnp.maximum(margin, 0))
    shifted = jax.random.randint(jax.random.fold_in(own, 4), (count // 2,), 0, 1 << 20) % (margin + 1)
    sizes = sizes.at[donor].add(-shifted).at[taker].add(shifted)
    members = jnp.searchsorted(jnp.cumsum(sizes), jnp.arange(rows * top), side="right").astype(jnp.int32)
    grid = members.reshape(top, rows).T
    grid = grid[jax.random.permutation(jax.random.fold_in(own, 1), rows)]
    turn = jax.random.randint(jax.random.fold_in(own, 2), (rows, 1), 0, top)
    return jnp.take_along_axis(grid, (jnp.arange(top)[None, :] + turn) % top, axis=1)


def shares(amount, total, most, skew, full):
    portions = [(1 << 20) // math.isqrt(standing ** skew) + 1 for standing in range(1, amount + 1)]
    largest = most if full else min(most, max(-(-total // amount), total * portions[0] // sum(portions)))
    least = 1 if total - largest >= amount - 1 else 0
    holding, spare = [largest] + [least] * (amount - 1), total - largest - least * (amount - 1)
    while spare > 0:
        candidates = [i for i in range(1, amount) if holding[i] < largest] or [i for i in range(1, amount) if holding[i] < most]
        whole, budget = sum([portions[i] for i in candidates]), spare
        for i in candidates:
            addition = min(most - holding[i], max(1, budget * portions[i] // whole), spare)
            holding[i] = holding[i] + addition
            spare = spare - addition
    return np.array(holding)


def normal_values(own_key, extent, deviation, bound, cuts=(), held_as=jnp.bfloat16):
    gain = block_scale(own_key, extent, cuts, -0.22, 0.18) if cuts else 1.0
    values = jax.random.normal(own_key, extent, jnp.float32) * deviation * gain
    return jnp.minimum(jnp.maximum(values, -bound), bound).astype(held_as)


def setup_inputs(seed: int = 0) -> dict:
    seeds = jax.random.split(jax.random.key(seed), 6)
    positions = normal_values(seeds[0], (3, PARTICLES), 1.0, 6.0, ((1, 768),), jnp.float32)
    velocities = normal_values(seeds[1], (3, PARTICLES), 1.0, 6.0, ((1, 768),), jnp.float32)
    masses = jnp.clip(jnp.exp(math.log(2.0) - 2.3025851 * jax.random.uniform(seeds[2], (PARTICLES,), jnp.float32) ** block_scale(seeds[2], (PARTICLES,), ((0, 768),), -0.2, 0.2)), 0.2, 2.0)
    owner_cell_keys = jax.random.split(jax.random.fold_in(seeds[3], 1), PARTICLES // PART_DEV)
    owner_cell_turns = jax.random.permutation(jax.random.fold_in(seeds[3], 3), PARTICLES // PART_DEV)
    owner_cell = jax.vmap(lambda own, number: routed_block(jax.random.fold_in(seeds[3], 2), own, number, PART_DEV, NCELL, 1, SLOT, 2))(owner_cell_keys, owner_cell_turns).reshape((PARTICLES, 1))
    counts = draw_counts(jax.random.fold_in(seeds[5], 71), 0)
    return dict(positions=positions, velocities=velocities, masses=masses, owner_cell=owner_cell, counts=counts)


drift_step = 0.5
kick_step = 0.5
soften = 0.25
reach = 4.0
coupling = 0.25

def pair_accel(centre, others):
    separation = others[:3, None, :] - centre[:3, :, None]
    distance = lax.optimization_barrier(jnp.sum(separation * separation, axis=0))
    inverse = lax.rsqrt(distance + soften)
    weight = others[3][None, :] * jnp.exp(-distance / reach) * inverse * inverse * inverse
    return coupling * lax.optimization_barrier(jnp.sum(weight[None] * separation, axis=2))

def reference(positions, velocities, masses, owner_cell, counts):
    groups = N_SLAB * N_DOM
    lanes = TILE // N_DOM
    moved = positions + drift_step * velocities
    payload = jnp.concatenate([moved, masses[None, :], velocities], axis=0)
    per_device = payload.reshape(7, groups, PART_DEV).transpose(1, 0, 2)
    targets_all = owner_cell[:, 0].reshape(groups, PART_DEV)
    targets = N_DOM * CELLS

    def pack(pieces):
        rows_here, target, limit = pieces
        active = jnp.arange(PART_DEV, dtype=jnp.int32) < limit
        hits = ((target[:, None] == jnp.arange(targets, dtype=jnp.int32)[None, :]) & active[:, None]).astype(jnp.int32)
        ranking = lax.optimization_barrier(jnp.sum(jnp.cumsum(hits, axis=0) * hits, axis=1)) - 1
        place = jnp.where(active, target * lanes + ranking, targets * lanes).astype(jnp.int32)
        buffer = jnp.zeros((7, targets * lanes), jnp.float32).at[:, place].set(rows_here, mode='drop')
        return buffer.reshape(7, N_DOM, CELLS, lanes)
    sent = lax.map(pack, (per_device, targets_all, counts))
    ncell = N_DOM * CELLS
    sorted_rows = sent.reshape(N_SLAB, N_DOM, 7, N_DOM, CELLS, lanes).transpose(2, 0, 3, 4, 1, 5).reshape(7, N_SLAB, ncell, TILE)
    padded = jnp.pad(sorted_rows[:4], ((0, 0), (1, 1), (1, 1), (0, 0)), mode='wrap')

    def cell_accel(number):
        slab_index = number // ncell
        cell_index = number % ncell
        zero = jnp.zeros((), jnp.int32)
        block = lax.dynamic_slice(padded, (zero, slab_index, cell_index, zero), (4, 3, 3, TILE)).reshape(4, 9 * TILE)
        centre = lax.dynamic_slice(padded, (zero, slab_index + 1, cell_index + 1, zero), (4, 1, 1, TILE)).reshape(4, TILE)
        return pair_accel(centre, block)
    accel = lax.map(cell_accel, jnp.arange(N_SLAB * ncell, dtype=jnp.int32), batch_size=64)
    accel = accel.reshape(N_SLAB, ncell, 3, TILE).transpose(2, 0, 1, 3)
    occupied = (sorted_rows[3:4] > 0).astype(jnp.float32)
    accel = accel * occupied
    state = jnp.concatenate([sorted_rows[:4], sorted_rows[4:7] + kick_step * accel, accel], axis=0)
    buddy = jnp.roll(state, -(N_SLAB // 2), axis=1)
    return (state, buddy)
```

```python
import functools
import math

import jax
import jax.numpy as jnp
from jax import lax
from jax.experimental import pallas as pl
from jax.experimental.pallas import tpu as pltpu
from jax.sharding import PartitionSpec as P

CELLS = 64
TILE = 128
SLOT = 32
BLOCK = 256
GROUP = 4
PARTS = 3
UNROLL = 8
F32, BF16 = jnp.float32, jnp.bfloat16
MESH = pl.DeviceIdType.MESH

drift_step = 0.5
kick_step = 0.5
soften = 0.25
reach = 4.0
coupling = 0.25
KAP = math.sqrt(math.log2(math.e) / reach)
C0 = KAP * KAP * soften
SCALE = coupling * 2.0**C0 * KAP**2


def rounded(x):
    return x.astype(BF16).astype(F32)


def place_rows(pos_ref, vel_ref, mass_ref, own_ref, cnt_ref, a_ref, b_ref, d_ref):
    rows = pos_ref.shape[1]
    before = lax.broadcasted_iota(jnp.int32, (BLOCK, BLOCK), 0) < lax.broadcasted_iota(jnp.int32, (BLOCK, BLOCK), 1)
    tri = jnp.concatenate([before.astype(BF16), jnp.ones((BLOCK, 128), BF16)], axis=1)
    owner = lax.broadcasted_iota(jnp.int32, (256, BLOCK), 0)
    ranks = lax.broadcasted_iota(jnp.int32, (SLOT, BLOCK), 0).astype(F32)
    lane = lax.broadcasted_iota(jnp.int32, (1, BLOCK), 1)
    live = cnt_ref[0]
    d_ref[...] = jnp.zeros_like(d_ref)

    def group(g, prefix):
        for q in range(GROUP):
            off = pl.multiple_of((g * GROUP + q) * BLOCK, BLOCK)
            here = pl.ds(q * BLOCK, BLOCK)
            hot = owner == jnp.where(lane + off < live, own_ref[:, pl.ds(off, BLOCK)], -1)
            hot16 = jnp.where(hot, 1.0, 0.0).astype(BF16)
            b_ref[:, here] = hot16
            seen = jnp.dot(hot16, tri, preferred_element_type=F32)
            earlier = seen[:, :BLOCK] + jnp.concatenate([prefix, prefix], axis=1)
            prefix = prefix + seen[:, BLOCK:]
            rank = ranks == jnp.sum(jnp.where(hot, earlier, 0.0), axis=0, keepdims=True)
            v = vel_ref[:, pl.ds(off, BLOCK)]
            x = pos_ref[:, pl.ds(off, BLOCK)] + drift_step * v
            values = [x[0:1], x[1:2], x[2:3], mass_ref[:, pl.ds(off, BLOCK)], v[0:1], v[1:2], v[2:3]]
            for c, value in enumerate(values):
                for piece in range(PARTS):
                    head = rounded(value)
                    a_ref[pl.ds((piece * 7 + c) * SLOT, SLOT), here] = jnp.where(rank, head, 0.0).astype(BF16)
                    value = value - head
        d_ref[...] += lax.dot_general(a_ref[...], b_ref[...], (((1,), (1,)), ((), ())), preferred_element_type=F32)
        return prefix

    lax.fori_loop(0, rows // (GROUP * BLOCK), group, jnp.zeros((256, 128), F32))


def kernel(
    n_slab, n_dom,
    pos_ref, vel_ref, mass_ref, own_ref, cnt_ref, state_ref, buddy_ref,
    a_ref, b_ref, d_ref, sent_ref, got_ref, x_ref, edge_out, edge_in, v_ref, ac_ref, bx_ref, bv_ref, ba_ref,
    xi_ref, j_ref, w_ref, tt_ref, je_ref, we_ref, te_ref, acc_ref, lb_ref,
    route_s, route_r, halo_s, halo_r, edge_s, edge_r, early_s, early_r, late_s, late_r,
):
    s, p = lax.axis_index("slab"), lax.axis_index("dom")
    up, down = lax.rem(s + 1, n_slab), lax.rem(s + n_slab - 1, n_slab)
    right, left = lax.rem(p + 1, n_dom), lax.rem(p + n_dom - 1, n_dom)
    other = lax.rem(s + n_slab // 2, n_slab)

    barrier = pltpu.get_barrier_semaphore()
    peers = [(s, lax.rem(p + t, n_dom)) for t in range(1, n_dom)]
    peers += [(a, b) for a in (up, down) for b in (p, left, right)]
    peers += [(other, p)]
    for peer in peers:
        pl.semaphore_signal(barrier, inc=1, device_id=peer, device_id_type=MESH)

    place_rows(pos_ref, vel_ref, mass_ref, own_ref, cnt_ref, a_ref, b_ref, d_ref)
    placed = d_ref[0:224]
    for piece in range(1, PARTS):
        placed = placed + d_ref[piece * 224 : piece * 224 + 224]
    for half in range(2):
        cols = slice(half * 128, half * 128 + 128)
        first = placed[0:128, cols].T
        second = jnp.concatenate([placed[128:224, cols], jnp.zeros((32, 128), F32)], axis=0).T
        sent_ref[0, cols] = pltpu.roll(first, p * SLOT, 1)
        sent_ref[1, cols] = pltpu.roll(second, p * SLOT, 1)

    pl.semaphore_wait(barrier, len(peers))

    def remote(src, dst, send, recv, device):
        return pltpu.make_async_remote_copy(
            src_ref=src, dst_ref=dst, send_sem=send, recv_sem=recv, device_id=device, device_id_type=MESH
        )

    route = [[], []]
    for half in range(2):
        for t in range(1, n_dom):
            q = lax.rem(p + t, n_dom)
            copy = remote(
                sent_ref.at[half, pl.ds(pl.multiple_of(q * CELLS, CELLS), CELLS)], got_ref.at[half, t - 1],
                route_s.at[half, t - 1], route_r.at[half, t - 1], (s, q),
            )
            copy.start()
            route[half].append(copy)

    acc_ref[...] = jnp.zeros_like(acc_ref)
    xi_ref[...] = jnp.full(xi_ref.shape, C0, F32)
    xi_ref[4] = jnp.zeros(xi_ref.shape[1:], F32)
    edge_out[...] = jnp.zeros_like(edge_out)
    je_ref[...] = jnp.zeros_like(je_ref)
    lane_group = lax.broadcasted_iota(jnp.int32, (CELLS, TILE), 1) // SLOT

    def merged(half, count):
        pieces = [(p, sent_ref[half, pl.ds(pl.multiple_of(p * CELLS, CELLS), CELLS)])]
        for t in range(1, n_dom):
            route[half][t - 1].wait_recv()
            pieces.append((lax.rem(p + n_dom - t, n_dom), got_ref[half, t - 1]))
        out = []
        for c in range(count):
            full = jnp.zeros((CELLS, TILE), F32)
            for source, piece in pieces:
                full = jnp.where(lane_group == lax.rem(source + c, n_dom), piece, full)
            out.append(full if c == 0 else pltpu.roll(full, TILE - c * SLOT, 1))
        return out

    own = merged(0, 4)
    for c in range(4):
        x_ref[0, c] = own[c]
        edge_out[0, c : c + 1] = own[c][0:1]
        edge_out[1, c : c + 1] = own[c][CELLS - 1 : CELLS]
    halo = [
        remote(x_ref.at[0], x_ref.at[k + 1], halo_s.at[k], halo_r.at[k], (to, p)) for k, to in enumerate((up, down))
    ]
    edges = []
    for side, to_dom, source in ((0, right, 1), (1, left, 0)):
        for k, to_slab in enumerate((s, up, down)):
            e = side * 3 + k
            edges.append(remote(edge_out.at[source], edge_in.at[e], edge_s.at[e], edge_r.at[e], (to_slab, to_dom)))
    early = [remote(x_ref.at[0], bx_ref, early_s.at[0], early_r.at[0], (other, p))]
    for copy in halo + edges + early:
        copy.start()

    def prepare(k):
        xs = [x_ref[k, c] * KAP for c in range(3)]
        m = x_ref[k, 3]
        n = xs[0] * xs[0] + xs[1] * xs[1] + xs[2] * xs[2]
        if k == 0:
            inner = pl.ds(8, CELLS)
            for c in range(3):
                xi_ref[c, inner] = xs[c]
            xi_ref[3, inner] = n + C0
            xi_ref[4, inner] = m
        for c, row in enumerate([xs[0] * -2.0, xs[1] * -2.0, xs[2] * -2.0, n]):
            j_ref[pl.ds(c, CELLS, stride=8), :] = row
            j_ref[pl.ds(c + 4, CELLS, stride=8), :] = row
        for c, row in enumerate([xs[0] * m, xs[1] * m, xs[2] * m, m]):
            head = rounded(row)
            w_ref[k, pl.ds(c, CELLS, stride=8), :] = head
            w_ref[k, pl.ds(c + 4, CELLS, stride=8), :] = row - head
        for g in range(CELLS // 16):
            tt_ref[k, g] = j_ref[pl.ds(g * 128, 128), :].T

    zero8 = jnp.zeros((8, TILE), F32)

    def spread(table, base, slot):
        for c in range(4):
            lb_ref[slot, c] = jnp.take_along_axis(table, jnp.full((TILE, TILE), base + c, jnp.int32), axis=1)

    def stage(k, n, slot):
        spread(tt_ref[k, n // 16], lax.rem(n, 16) * 8, slot)

    def pairs(weights, slot, centres):
        weights = jnp.concatenate([weights, zero8], axis=0).astype(BF16)
        ax, ay, az, nj = [lb_ref[slot, c] for c in range(4)]
        for i in centres:
            x, y, z, n = [xi_ref[c, pl.ds(i + 8, 1), :] for c in range(4)]
            u = ((ax * x + ay * y) + (az * z + nj)) + n
            w = jnp.exp2(jnp.log2(u) * -1.5 - u)
            head = w.astype(BF16)
            rest = (w - head.astype(F32)).astype(BF16)
            pull = jnp.dot(weights, head, preferred_element_type=F32) + jnp.dot(weights, rest, preferred_element_type=F32)
            acc_ref[pl.ds(pl.multiple_of((i + 9) * 8, 8), 8), :] += pull[:8]

    def cell(k, n, slot):
        pairs(w_ref[k, pl.ds(pl.multiple_of(n * 8, 8), 8), :], slot, (n - 1, n, n + 1))

    prepare(0)
    stage(0, 0, 0)

    def inner_slab(step, carry):
        for i in range(UNROLL):
            n = step * UNROLL + i
            stage(0, jnp.minimum(n + 1, CELLS - 1), (i + 1) % UNROLL)
            cell(0, n, i)
        return carry

    lax.fori_loop(0, CELLS // UNROLL, inner_slab, 0)

    speed = merged(1, 3)
    for c in range(3):
        v_ref[c] = speed[c]
    early.append(remote(v_ref, bv_ref, early_s.at[1], early_r.at[1], (other, p)))
    early[1].start()

    for e, copy in enumerate(edges):
        copy.wait_recv()
        tile = edge_in[e]
        xs = [tile[c : c + 1] * KAP for c in range(3)]
        m = tile[3:4]
        n = xs[0] * xs[0] + xs[1] * xs[1] + xs[2] * xs[2]
        for c, row in enumerate([xs[0] * -2.0, xs[1] * -2.0, xs[2] * -2.0, n]):
            je_ref[e * 8 + c : e * 8 + c + 1] = row
        for c, row in enumerate([xs[0] * m, xs[1] * m, xs[2] * m, m]):
            head = rounded(row)
            we_ref[e * 8 + c : e * 8 + c + 1] = head
            we_ref[e * 8 + c + 4 : e * 8 + c + 5] = row - head
    te_ref[...] = je_ref[...].T
    for e in range(6):
        spread(te_ref[...], e * 8, e)
        pairs(we_ref[e * 8 : e * 8 + 8], e, (0 if e < 3 else CELLS - 1,))

    for k, copy in enumerate(halo):
        copy.wait_recv()
        prepare(k + 1)

    def finish(row):
        total = []
        for c in range(4):
            at = pl.multiple_of((row + 1) * 8, 8)
            total.append(acc_ref[pl.ds(at + c, 8, stride=8), :] + acc_ref[pl.ds(at + c + 4, 8, stride=8), :])
        live = xi_ref[4, pl.ds(row, 8)] > 0
        for c in range(3):
            pull = (total[c] - xi_ref[c, pl.ds(row, 8)] * total[3]) * SCALE
            ac_ref[c, pl.ds(row, 8)] = jnp.where(live, pull, 0.0)

    def late(k, rows):
        part = pl.ds(pl.multiple_of(k * 16, 8), rows)
        return remote(ac_ref.at[:, part], ba_ref.at[:, part], late_s.at[k], late_r.at[k], (other, p))

    per_step = UNROLL // 2
    stage(1, 0, 0)

    def chunk(k, carry):
        def outer_slabs(step, carry):
            for i in range(per_step):
                n = k * 16 + step * per_step + i
                stage(2, n, (2 * i + 1) % UNROLL)
                cell(1, n, 2 * i)
                stage(1, jnp.minimum(n + 1, CELLS - 1), (2 * i + 2) % UNROLL)
                cell(2, n, 2 * i + 1)
            return carry

        lax.fori_loop(0, 16 // per_step, outer_slabs, 0)
        row = pl.multiple_of(k * 16, 8)
        finish(row)
        finish(row + 8)
        late(k, 16).start()
        return carry

    lax.fori_loop(0, CELLS // 16, chunk, 0)
    finish(CELLS)
    last = CELLS // 16
    late(last, 8).start()

    state_ref[0:4] = x_ref[0]
    accel = ac_ref[:, 8:]
    state_ref[4:7] = v_ref[...] + kick_step * accel
    state_ref[7:10] = accel
    for copy in early:
        copy.wait_recv()
    for k in range(last + 1):
        late(k, 16 if k < last else 8).wait_recv()
    buddy_ref[0:4] = bx_ref[...]
    accel = ba_ref[:, 8:]
    buddy_ref[4:7] = bv_ref[...] + kick_step * accel
    buddy_ref[7:10] = accel
    for copy in route[0] + route[1] + halo + edges + early:
        copy.wait_send()
    for k in range(last + 1):
        late(k, 16 if k < last else 8).wait_send()


def per_device(positions, velocities, masses, owner_cell, counts):
    n_slab, n_dom = lax.axis_size("slab"), lax.axis_size("dom")
    vmem = pl.BlockSpec(memory_space=pltpu.VMEM)
    out = jax.ShapeDtypeStruct((10, CELLS, TILE), F32)
    block = (CELLS, TILE)
    dma = pltpu.SemaphoreType.DMA
    state, buddy = pl.pallas_call(
        functools.partial(kernel, n_slab, n_dom),
        out_shape=(out, out),
        in_specs=[vmem] * 4 + [pl.BlockSpec(memory_space=pltpu.SMEM)],
        out_specs=(vmem, vmem),
        scratch_shapes=[
            pltpu.VMEM((PARTS * 224, GROUP * BLOCK), BF16),
            pltpu.VMEM((256, GROUP * BLOCK), BF16),
            pltpu.VMEM((PARTS * 224, 256), F32),
            pltpu.VMEM((2, 256, 128), F32),
            pltpu.VMEM((2, 3, *block), F32),
            pltpu.VMEM((3, 4, *block), F32),
            pltpu.VMEM((2, 8, TILE), F32),
            pltpu.VMEM((6, 8, TILE), F32),
            pltpu.VMEM((3, *block), F32),
            pltpu.VMEM((3, CELLS + 8, TILE), F32),
            pltpu.VMEM((4, *block), F32),
            pltpu.VMEM((3, *block), F32),
            pltpu.VMEM((3, CELLS + 8, TILE), F32),
            pltpu.VMEM((5, CELLS + 16, TILE), F32),
            pltpu.VMEM((CELLS * 8, TILE), F32),
            pltpu.VMEM((3, CELLS * 8, TILE), F32),
            pltpu.VMEM((3, CELLS // 16, TILE, TILE), F32),
            pltpu.VMEM((TILE, TILE), F32),
            pltpu.VMEM((48, TILE), F32),
            pltpu.VMEM((TILE, TILE), F32),
            pltpu.VMEM(((CELLS + 10) * 8, TILE), F32),
            pltpu.VMEM((UNROLL, 4, TILE, TILE), F32),
            dma((2, 3)), dma((2, 3)), dma((2,)), dma((2,)), dma((6,)), dma((6,)), dma((2,)), dma((2,)), dma((5,)), dma((5,)),
        ],
        compiler_params=pltpu.CompilerParams(collective_id=0, has_side_effects=True),
        name="substep",
    )(positions, velocities, masses.reshape(1, -1), owner_cell.reshape(1, -1), counts)
    return state[:, None], buddy[:, None]


def solution(mesh):
    placed = (
        P(None, ("slab", "dom")),
        P(None, ("slab", "dom")),
        P(("slab", "dom")),
        P(("slab", "dom"), None),
        P(("slab", "dom")),
    )
    return jax.shard_map(
        per_device,
        mesh=mesh,
        in_specs=placed,
        out_specs=(P(None, "slab", "dom", None), P(None, "slab", "dom", None)),
        check_vma=False,
    )
```

```python
import functools
import math

import jax
import jax.numpy as jnp
from jax import lax
from jax.experimental import pallas as pl
from jax.experimental.pallas import tpu as pltpu
from jax.sharding import PartitionSpec as P

CELLS = 64
TILE = 128
SLOT = 32
BLOCK = 256
GROUP = 8
PARTS = 2
UNROLL = 16
VMEM_LIMIT = 24 << 20
DELAY = 2
FAR = 8
F32, BF16 = jnp.float32, jnp.bfloat16
MESH = pl.DeviceIdType.MESH

drift_step = 0.5
kick_step = 0.5
soften = 0.25
reach = 4.0
coupling = 0.25
KAP = math.sqrt(math.log2(math.e) / reach)
C0 = KAP * KAP * soften
SCALE = coupling * 2.0**C0 * KAP**2


def rounded(x):
    return x.astype(BF16).astype(F32)


def place_rows(pos_ref, vel_ref, mass_ref, own_ref, cnt_ref, a_ref, av_ref, b_ref, d_ref):
    rows = pos_ref.shape[1]
    before = lax.broadcasted_iota(jnp.int32, (BLOCK, BLOCK), 0) < lax.broadcasted_iota(jnp.int32, (BLOCK, BLOCK), 1)
    tri = jnp.concatenate([before.astype(BF16), jnp.ones((BLOCK, 128), BF16)], axis=1)
    owner = lax.broadcasted_iota(jnp.int32, (256, BLOCK), 0)
    ranks = lax.broadcasted_iota(jnp.int32, (SLOT, BLOCK), 0).astype(F32)
    lane = lax.broadcasted_iota(jnp.int32, (1, BLOCK), 1)
    live = cnt_ref[0]
    d_ref[...] = jnp.zeros_like(d_ref)

    def group(g, prefix):
        whole = pl.ds(pl.multiple_of(g * GROUP * BLOCK, BLOCK), GROUP * BLOCK)
        for q in range(GROUP):
            off = pl.multiple_of((g * GROUP + q) * BLOCK, BLOCK)
            rows_here = pl.ds(off, BLOCK)
            hot = owner == jnp.where(lane + off < live, own_ref[:, rows_here], -1)
            hot16 = jnp.where(hot, 1.0, 0.0).astype(BF16)
            b_ref[:, rows_here] = hot16
            seen = jnp.dot(hot16, tri, preferred_element_type=F32)
            earlier = seen[:, :BLOCK] + jnp.concatenate([prefix, prefix], axis=1)
            prefix = prefix + seen[:, BLOCK:]
            rank = ranks == jnp.sum(jnp.where(hot, earlier, 0.0), axis=0, keepdims=True)

            def put(ref, values, where):
                for c, value in enumerate(values):
                    for piece in range(PARTS):
                        head = rounded(value)
                        at = pl.ds((piece * len(values) + c) * SLOT, SLOT)
                        ref[at, where] = jnp.where(rank, head, 0.0).astype(BF16)
                        value = value - head

            v = vel_ref[:, rows_here]
            x = pos_ref[:, rows_here] + drift_step * v
            put(a_ref, [x[0:1], x[1:2], x[2:3], mass_ref[:, rows_here]], pl.ds(q * BLOCK, BLOCK))
            put(av_ref, [v[0:1], v[1:2], v[2:3]], rows_here)
        d_ref[...] += product(a_ref[...], b_ref[:, whole])
        return prefix

    lax.fori_loop(0, rows // (GROUP * BLOCK), group, jnp.zeros((256, 128), F32))


def product(a, b):
    return lax.dot_general(a, b, (((1,), (1,)), ((), ())), preferred_element_type=F32)


def summed(pieces, size):
    total = pieces[0:size]
    for piece in range(1, PARTS):
        total = total + pieces[piece * size : (piece + 1) * size]
    return total


def kernel(
    n_slab, n_dom,
    pos_ref, vel_ref, mass_ref, own_ref, cnt_ref, state_ref, buddy_ref,
    a_ref, av_ref, b_ref, d_ref, sent_ref, got_ref, x_ref, edge_out, edge_in, v_ref, ac_ref, bx_ref, bv_ref, ba_ref,
    sv_ref, bw_ref, xi_ref, j_ref, w_ref, tt_ref, je_ref, we_ref, te_ref, acc_ref, lb_ref,
    route_s, route_r, halo_s, halo_r, edge_s, edge_r, early_s, early_r, late_s, late_r, out_s,
):
    s, p = lax.axis_index("slab"), lax.axis_index("dom")
    up, down = lax.rem(s + 1, n_slab), lax.rem(s + n_slab - 1, n_slab)
    right, left = lax.rem(p + 1, n_dom), lax.rem(p + n_dom - 1, n_dom)
    other = lax.rem(s + n_slab // 2, n_slab)

    barrier = pltpu.get_barrier_semaphore()
    peers = [(s, lax.rem(p + t, n_dom)) for t in range(1, n_dom)]
    peers += [(a, b) for a in (up, down) for b in (p, left, right)]
    peers += [(other, p)]
    for peer in peers:
        pl.semaphore_signal(barrier, inc=1, device_id=peer, device_id_type=MESH)

    place_rows(pos_ref, vel_ref, mass_ref, own_ref, cnt_ref, a_ref, av_ref, b_ref, d_ref)

    def pack(half, placed):
        for cols in (slice(0, 128), slice(128, 256)):
            sent_ref[half, cols] = pltpu.roll(placed[:, cols].T, p * SLOT, 1)

    pack(0, summed(d_ref[...], 4 * SLOT))
    pl.semaphore_wait(barrier, len(peers))

    def remote(src, dst, send, recv, device):
        return pltpu.make_async_remote_copy(
            src_ref=src, dst_ref=dst, send_sem=send, recv_sem=recv, device_id=device, device_id_type=MESH
        )

    route = [[], []]

    def send_rows(half):
        for t in range(1, n_dom):
            q = lax.rem(p + t, n_dom)
            copy = remote(
                sent_ref.at[half, pl.ds(pl.multiple_of(q * CELLS, CELLS), CELLS)], got_ref.at[half, t - 1],
                route_s.at[half, t - 1], route_r.at[half, t - 1], (s, q),
            )
            copy.start()
            route[half].append(copy)

    send_rows(0)
    speeds = summed(product(av_ref[...], b_ref[...]), 3 * SLOT)
    pack(1, jnp.concatenate([speeds, jnp.zeros((SLOT, 256), F32)], axis=0))
    send_rows(1)
    acc_ref[...] = jnp.zeros_like(acc_ref)
    xi_ref[...] = jnp.full(xi_ref.shape, C0, F32)
    xi_ref[4] = jnp.zeros(xi_ref.shape[1:], F32)
    edge_out[...] = jnp.zeros_like(edge_out)
    je_ref[...] = jnp.zeros_like(je_ref)
    lane_group = lax.broadcasted_iota(jnp.int32, (CELLS, TILE), 1) // SLOT

    def merged(half, count):
        pieces = [(p, sent_ref[half, pl.ds(pl.multiple_of(p * CELLS, CELLS), CELLS)])]
        for t in range(1, n_dom):
            route[half][t - 1].wait_recv()
            pieces.append((lax.rem(p + n_dom - t, n_dom), got_ref[half, t - 1]))
        out = []
        for c in range(count):
            full = jnp.zeros((CELLS, TILE), F32)
            for source, piece in pieces:
                full = jnp.where(lane_group == lax.rem(source + c, n_dom), piece, full)
            out.append(full if c == 0 else pltpu.roll(full, TILE - c * SLOT, 1))
        return out

    own = merged(0, 4)
    for c in range(4):
        x_ref[0, c] = own[c]
        edge_out[0, c : c + 1] = own[c][0:1]
        edge_out[1, c : c + 1] = own[c][CELLS - 1 : CELLS]
    halo = [
        remote(x_ref.at[0], x_ref.at[k + 1], halo_s.at[k], halo_r.at[k], (to, p)) for k, to in enumerate((up, down))
    ]
    edges = []
    for side, to_dom, source in ((0, right, 1), (1, left, 0)):
        for k, to_slab in enumerate((s, up, down)):
            e = side * 3 + k
            edges.append(remote(edge_out.at[source], edge_in.at[e], edge_s.at[e], edge_r.at[e], (to_slab, to_dom)))
    for copy in halo + edges:
        copy.start()
    outs = [pltpu.make_async_copy(x_ref.at[0], state_ref.at[0:4], out_s.at[0])]
    outs[0].start()
    early = [remote(x_ref.at[0], bx_ref, early_s.at[0], early_r.at[0], (other, p))]
    crossing = lax.rem(s + 2, 2 * FAR) < 4
    turn = jnp.where(crossing, DELAY, 0)

    def prepare(k):
        xs = [x_ref[k, c] * KAP for c in range(3)]
        m = x_ref[k, 3]
        n = xs[0] * xs[0] + xs[1] * xs[1] + xs[2] * xs[2]
        if isinstance(k, int):
            inner = pl.ds(8, CELLS)
            for c in range(3):
                xi_ref[c, inner] = xs[c]
            xi_ref[3, inner] = n + C0
            xi_ref[4, inner] = m
        for c, row in enumerate([xs[0] * -2.0, xs[1] * -2.0, xs[2] * -2.0, n]):
            j_ref[pl.ds(c, CELLS, stride=8), :] = row
            j_ref[pl.ds(c + 4, CELLS, stride=8), :] = row
        for c, row in enumerate([xs[0] * m, xs[1] * m, xs[2] * m, m]):
            head = rounded(row)
            w_ref[k, pl.ds(c, CELLS, stride=8), :] = head
            w_ref[k, pl.ds(c + 4, CELLS, stride=8), :] = row - head
        for g in range(CELLS // 16):
            tt_ref[k, g] = j_ref[pl.ds(g * 128, 128), :].T

    zero8 = jnp.zeros((8, TILE), F32)

    def spread(table, base, slot):
        for c in range(4):
            lb_ref[slot, c] = jnp.take_along_axis(table, jnp.full((TILE, TILE), base + c, jnp.int32), axis=1)

    def stage(k, n, slot):
        spread(tt_ref[k, n // 16], lax.rem(n, 16) * 8, slot)

    def pairs(weights, slot, centres):
        weights = jnp.concatenate([weights, zero8], axis=0).astype(BF16)
        ax, ay, az, nj = [lb_ref[slot, c] for c in range(4)]
        for i in centres:
            x, y, z, n = [xi_ref[c, pl.ds(i + 8, 1), :] for c in range(4)]
            u = ((ax * x + ay * y) + (az * z + nj)) + n
            w = jnp.exp2(jnp.log2(u) * -1.5 - u)
            head = w.astype(BF16)
            rest = (w - head.astype(F32)).astype(BF16)
            pull = jnp.dot(weights, head, preferred_element_type=F32) + jnp.dot(weights, rest, preferred_element_type=F32)
            acc_ref[pl.ds(pl.multiple_of((i + 9) * 8, 8), 8), :] += pull[:8]

    def cell(k, n, slot):
        pairs(w_ref[k, pl.ds(pl.multiple_of(n * 8, 8), 8), :], slot, (n - 1, n, n + 1))

    def whole_slab(k, own=False):
        def step(t, carry):
            if own:

                @pl.when(t == turn)
                def _():
                    early[0].start()

            for i in range(UNROLL):
                n = t * UNROLL + i
                stage(k, jnp.minimum(n + 1, CELLS - 1), (i + 1) % UNROLL)
                cell(k, n, i)
            return carry

        stage(k, 0, 0)
        lax.fori_loop(0, CELLS // UNROLL, step, 0)

    prepare(0)
    whole_slab(0, own=True)

    speed = merged(1, 3)
    for c in range(3):
        v_ref[c] = speed[c]
    early.append(remote(v_ref, bv_ref, early_s.at[1], early_r.at[1], (other, p)))
    early[1].start()

    near = jnp.where(lax.rem(s, FAR) == 0, 2, 1)
    far = 3 - near

    def arrived(k):
        remote(x_ref.at[0], x_ref.at[k], halo_s.at[k - 1], halo_r.at[k - 1], (up, p)).wait_recv()

    arrived(near)
    prepare(near)
    whole_slab(near)

    for e, copy in enumerate(edges):
        copy.wait_recv()
        tile = edge_in[e]
        xs = [tile[c : c + 1] * KAP for c in range(3)]
        m = tile[3:4]
        n = xs[0] * xs[0] + xs[1] * xs[1] + xs[2] * xs[2]
        for c, row in enumerate([xs[0] * -2.0, xs[1] * -2.0, xs[2] * -2.0, n]):
            je_ref[e * 8 + c : e * 8 + c + 1] = row
        for c, row in enumerate([xs[0] * m, xs[1] * m, xs[2] * m, m]):
            head = rounded(row)
            we_ref[e * 8 + c : e * 8 + c + 1] = head
            we_ref[e * 8 + c + 4 : e * 8 + c + 5] = row - head
    te_ref[...] = je_ref[...].T
    for e in range(6):
        spread(te_ref[...], e * 8, e)
        pairs(we_ref[e * 8 : e * 8 + 8], e, (0 if e < 3 else CELLS - 1,))

    arrived(far)
    prepare(far)

    def finish(row):
        total = []
        for c in range(4):
            at = pl.multiple_of((row + 1) * 8, 8)
            total.append(acc_ref[pl.ds(at + c, 8, stride=8), :] + acc_ref[pl.ds(at + c + 4, 8, stride=8), :])
        live = xi_ref[4, pl.ds(row, 8)] > 0
        for c in range(3):
            pull = (total[c] - xi_ref[c, pl.ds(row, 8)] * total[3]) * SCALE
            ac_ref[c, pl.ds(row, 8)] = jnp.where(live, pull, 0.0)

    def late(k, rows):
        part = pl.ds(pl.multiple_of(k * 16, 8), rows)
        return remote(ac_ref.at[:, part], ba_ref.at[:, part], late_s.at[k], late_r.at[k], (other, p))

    stage(far, 0, 0)

    def chunk(k, carry):
        def step(t, carry):
            for i in range(UNROLL):
                n = k * 16 + t * UNROLL + i
                stage(far, jnp.minimum(n + 1, CELLS - 1), (i + 1) % UNROLL)
                cell(far, n, i)
            return carry

        lax.fori_loop(0, 16 // UNROLL, step, 0)
        row = pl.multiple_of(k * 16, 8)
        finish(row)
        finish(row + 8)
        late(k, 16).start()
        return carry

    lax.fori_loop(0, CELLS // 16, chunk, 0)
    finish(CELLS)
    last = CELLS // 16
    late(last, 8).start()

    def store(src, dst):
        outs.append(pltpu.make_async_copy(src, dst, out_s.at[len(outs)]))
        outs[-1].start()

    inner = pl.ds(8, CELLS)
    sv_ref[...] = v_ref[...] + kick_step * ac_ref[:, inner]
    store(sv_ref, state_ref.at[4:7])
    store(ac_ref.at[:, inner], state_ref.at[7:10])
    for copy in early:
        copy.wait_recv()
    store(bx_ref, buddy_ref.at[0:4])
    for k in range(last + 1):
        late(k, 16 if k < last else 8).wait_recv()
    store(ba_ref.at[:, inner], buddy_ref.at[7:10])
    bw_ref[...] = bv_ref[...] + kick_step * ba_ref[:, inner]
    store(bw_ref, buddy_ref.at[4:7])
    for copy in outs:
        copy.wait()
    for copy in route[0] + route[1] + halo + edges + early:
        copy.wait_send()
    for k in range(last + 1):
        late(k, 16 if k < last else 8).wait_send()


def per_device(positions, velocities, masses, owner_cell, counts):
    n_slab, n_dom = lax.axis_size("slab"), lax.axis_size("dom")
    rows = positions.shape[1]
    vmem = pl.BlockSpec(memory_space=pltpu.VMEM)
    out = jax.ShapeDtypeStruct((10, CELLS, TILE), F32)
    block = (CELLS, TILE)
    dma = pltpu.SemaphoreType.DMA
    state, buddy = pl.pallas_call(
        functools.partial(kernel, n_slab, n_dom),
        out_shape=(out, out),
        in_specs=[vmem] * 4 + [pl.BlockSpec(memory_space=pltpu.SMEM)],
        out_specs=(pl.BlockSpec(memory_space=pl.ANY),) * 2,
        scratch_shapes=[
            pltpu.VMEM((PARTS * 4 * SLOT, GROUP * BLOCK), BF16),
            pltpu.VMEM((PARTS * 3 * SLOT, rows), BF16),
            pltpu.VMEM((256, rows), BF16),
            pltpu.VMEM((PARTS * 4 * SLOT, 256), F32),
            pltpu.VMEM((2, 256, 128), F32),
            pltpu.VMEM((2, 3, *block), F32),
            pltpu.VMEM((3, 4, *block), F32),
            pltpu.VMEM((2, 8, TILE), F32),
            pltpu.VMEM((6, 8, TILE), F32),
            pltpu.VMEM((3, *block), F32),
            pltpu.VMEM((3, CELLS + 8, TILE), F32),
            pltpu.VMEM((4, *block), F32),
            pltpu.VMEM((3, *block), F32),
            pltpu.VMEM((3, CELLS + 8, TILE), F32),
            pltpu.VMEM((3, *block), F32),
            pltpu.VMEM((3, *block), F32),
            pltpu.VMEM((5, CELLS + 16, TILE), F32),
            pltpu.VMEM((CELLS * 8, TILE), F32),
            pltpu.VMEM((3, CELLS * 8, TILE), F32),
            pltpu.VMEM((3, CELLS // 16, TILE, TILE), F32),
            pltpu.VMEM((TILE, TILE), F32),
            pltpu.VMEM((48, TILE), F32),
            pltpu.VMEM((TILE, TILE), F32),
            pltpu.VMEM(((CELLS + 10) * 8, TILE), F32),
            pltpu.VMEM((UNROLL, 4, TILE, TILE), F32),
            dma((2, 3)), dma((2, 3)), dma((2,)), dma((2,)), dma((6,)), dma((6,)), dma((2,)), dma((2,)), dma((5,)), dma((5,)), dma((6,)),
        ],
        compiler_params=pltpu.CompilerParams(collective_id=0, has_side_effects=True, vmem_limit_bytes=VMEM_LIMIT),
        name="substep",
    )(positions, velocities, masses.reshape(1, -1), owner_cell.reshape(1, -1), counts)
    return state[:, None], buddy[:, None]


def solution(mesh):
    placed = (
        P(None, ("slab", "dom")),
        P(None, ("slab", "dom")),
        P(("slab", "dom")),
        P(("slab", "dom"), None),
        P(("slab", "dom")),
    )
    return jax.shard_map(
        per_device,
        mesh=mesh,
        in_specs=placed,
        out_specs=(P(None, "slab", "dom", None), P(None, "slab", "dom", None)),
        check_vma=False,
    )
```

```python
import functools
import math

import jax
import jax.numpy as jnp
from jax import lax
from jax.experimental import pallas as pl
from jax.experimental.pallas import tpu as pltpu
from jax.sharding import PartitionSpec as P

CELLS = 64
TILE = 128
SLOT = 32
BLOCK = 256
GROUP = 8
PARTS = 2
UNROLL = 16
VMEM_LIMIT = 24 << 20
DELAY = 2
FAR = 8
F32, BF16 = jnp.float32, jnp.bfloat16
MESH = pl.DeviceIdType.MESH

drift_step = 0.5
kick_step = 0.5
soften = 0.25
reach = 4.0
coupling = 0.25
KAP = math.sqrt(math.log2(math.e) / reach)
C0 = KAP * KAP * soften
SCALE = coupling * 2.0**C0 * KAP**2


def rounded(x):
    return x.astype(BF16).astype(F32)


def place_rows(pos_ref, vel_ref, mass_ref, own_ref, cnt_ref, a_ref, av_ref, b_ref, d_ref):
    rows = pos_ref.shape[1]
    before = lax.broadcasted_iota(jnp.int32, (BLOCK, BLOCK), 0) < lax.broadcasted_iota(jnp.int32, (BLOCK, BLOCK), 1)
    tri = jnp.concatenate([before.astype(BF16), jnp.ones((BLOCK, 128), BF16)], axis=1)
    owner = lax.broadcasted_iota(jnp.int32, (256, BLOCK), 0)
    ranks = lax.broadcasted_iota(jnp.int32, (SLOT, BLOCK), 0).astype(F32)
    lane = lax.broadcasted_iota(jnp.int32, (1, BLOCK), 1)
    live = cnt_ref[0]
    d_ref[...] = jnp.zeros_like(d_ref)

    def group(g, prefix):
        whole = pl.ds(pl.multiple_of(g * GROUP * BLOCK, BLOCK), GROUP * BLOCK)
        for q in range(GROUP):
            off = pl.multiple_of((g * GROUP + q) * BLOCK, BLOCK)
            rows_here = pl.ds(off, BLOCK)
            hot = owner == jnp.where(lane + off < live, own_ref[:, rows_here], -1)
            hot16 = jnp.where(hot, 1.0, 0.0).astype(BF16)
            b_ref[:, rows_here] = hot16
            seen = jnp.dot(hot16, tri, preferred_element_type=F32)
            earlier = seen[:, :BLOCK] + jnp.concatenate([prefix, prefix], axis=1)
            prefix = prefix + seen[:, BLOCK:]
            rank = ranks == jnp.sum(jnp.where(hot, earlier, 0.0), axis=0, keepdims=True)

            def put(ref, values, where):
                for c, value in enumerate(values):
                    for piece in range(PARTS):
                        head = rounded(value)
                        at = pl.ds((piece * len(values) + c) * SLOT, SLOT)
                        ref[at, where] = jnp.where(rank, head, 0.0).astype(BF16)
                        value = value - head

            v = vel_ref[:, rows_here]
            x = pos_ref[:, rows_here] + drift_step * v
            put(a_ref, [x[0:1], x[1:2], x[2:3], mass_ref[:, rows_here]], pl.ds(q * BLOCK, BLOCK))
            put(av_ref, [v[0:1], v[1:2], v[2:3]], rows_here)
        d_ref[...] += product(a_ref[...], b_ref[:, whole])
        return prefix

    lax.fori_loop(0, rows // (GROUP * BLOCK), group, jnp.zeros((256, 128), F32))


def product(a, b):
    return lax.dot_general(a, b, (((1,), (1,)), ((), ())), preferred_element_type=F32)


def summed(pieces, size):
    total = pieces[0:size]
    for piece in range(1, PARTS):
        total = total + pieces[piece * size : (piece + 1) * size]
    return total


def kernel(
    n_slab, n_dom,
    pos_hbm, vel_hbm, mass_hbm, own_hbm, cnt_ref, state_ref, buddy_ref, pos_ref, vel_ref, mass_ref, own_ref,
    a_ref, av_ref, b_ref, d_ref, sent_ref, got_ref, x_ref, edge_out, edge_in, v_ref, ac_ref, bx_ref, bv_ref, ba_ref,
    sv_ref, bw_ref, xi_ref, j_ref, w_ref, tt_ref, je_ref, we_ref, te_ref, acc_ref, lb_ref,
    route_s, route_r, halo_s, halo_r, edge_s, edge_r, early_s, early_r, late_s, late_r, out_s, in_s,
):
    s, p = lax.axis_index("slab"), lax.axis_index("dom")
    up, down = lax.rem(s + 1, n_slab), lax.rem(s + n_slab - 1, n_slab)
    right, left = lax.rem(p + 1, n_dom), lax.rem(p + n_dom - 1, n_dom)
    other = lax.rem(s + n_slab // 2, n_slab)

    pairs_in = ((own_hbm, own_ref), (pos_hbm, pos_ref), (vel_hbm, vel_ref), (mass_hbm, mass_ref))
    loads = [pltpu.make_async_copy(src, dst, in_s.at[i]) for i, (src, dst) in enumerate(pairs_in)]
    for copy in loads:
        copy.start()
    barrier = pltpu.get_barrier_semaphore()
    peers = [(s, lax.rem(p + t, n_dom)) for t in range(1, n_dom)]
    peers += [(a, b) for a in (up, down) for b in (p, left, right)]
    peers += [(other, p)]
    for peer in peers:
        pl.semaphore_signal(barrier, inc=1, device_id=peer, device_id_type=MESH)

    acc_ref[...] = jnp.zeros_like(acc_ref)
    xi_ref[...] = jnp.full(xi_ref.shape, C0, F32)
    xi_ref[4] = jnp.zeros(xi_ref.shape[1:], F32)
    edge_out[...] = jnp.zeros_like(edge_out)
    je_ref[...] = jnp.zeros_like(je_ref)
    for copy in loads:
        copy.wait()
    place_rows(pos_ref, vel_ref, mass_ref, own_ref, cnt_ref, a_ref, av_ref, b_ref, d_ref)

    def pack(half, placed):
        for cols in (slice(0, 128), slice(128, 256)):
            sent_ref[half, cols] = pltpu.roll(placed[:, cols].T, p * SLOT, 1)

    pack(0, summed(d_ref[...], 4 * SLOT))
    pl.semaphore_wait(barrier, len(peers))

    def remote(src, dst, send, recv, device):
        return pltpu.make_async_remote_copy(
            src_ref=src, dst_ref=dst, send_sem=send, recv_sem=recv, device_id=device, device_id_type=MESH
        )

    route = [[], []]

    def send_rows(half):
        for t in range(1, n_dom):
            q = lax.rem(p + t, n_dom)
            copy = remote(
                sent_ref.at[half, pl.ds(pl.multiple_of(q * CELLS, CELLS), CELLS)], got_ref.at[half, t - 1],
                route_s.at[half, t - 1], route_r.at[half, t - 1], (s, q),
            )
            copy.start()
            route[half].append(copy)

    send_rows(0)
    speeds = summed(product(av_ref[...], b_ref[...]), 3 * SLOT)
    pack(1, jnp.concatenate([speeds, jnp.zeros((SLOT, 256), F32)], axis=0))
    send_rows(1)
    lane_group = lax.broadcasted_iota(jnp.int32, (CELLS, TILE), 1) // SLOT

    def merged(half, count):
        pieces = [(p, sent_ref[half, pl.ds(pl.multiple_of(p * CELLS, CELLS), CELLS)])]
        for t in range(1, n_dom):
            route[half][t - 1].wait_recv()
            pieces.append((lax.rem(p + n_dom - t, n_dom), got_ref[half, t - 1]))
        out = []
        for c in range(count):
            full = jnp.zeros((CELLS, TILE), F32)
            for source, piece in pieces:
                full = jnp.where(lane_group == lax.rem(source + c, n_dom), piece, full)
            out.append(full if c == 0 else pltpu.roll(full, TILE - c * SLOT, 1))
        return out

    own = merged(0, 4)
    for c in range(4):
        x_ref[0, c] = own[c]
        edge_out[0, c : c + 1] = own[c][0:1]
        edge_out[1, c : c + 1] = own[c][CELLS - 1 : CELLS]
    halo = [
        remote(x_ref.at[0], x_ref.at[k + 1], halo_s.at[k], halo_r.at[k], (to, p)) for k, to in enumerate((up, down))
    ]
    edges = []
    for side, to_dom, source in ((0, right, 1), (1, left, 0)):
        for k, to_slab in enumerate((s, up, down)):
            e = side * 3 + k
            edges.append(remote(edge_out.at[source], edge_in.at[e], edge_s.at[e], edge_r.at[e], (to_slab, to_dom)))
    for copy in halo + edges:
        copy.start()
    outs = [pltpu.make_async_copy(x_ref.at[0], state_ref.at[0:4], out_s.at[0])]
    outs[0].start()
    early = [remote(x_ref.at[0], bx_ref, early_s.at[0], early_r.at[0], (other, p))]
    crossing = lax.rem(s + 2, 2 * FAR) < 4
    turn = jnp.where(crossing, DELAY, 0)

    def prepare(k):
        xs = [x_ref[k, c] * KAP for c in range(3)]
        m = x_ref[k, 3]
        n = xs[0] * xs[0] + xs[1] * xs[1] + xs[2] * xs[2]
        if isinstance(k, int):
            inner = pl.ds(8, CELLS)
            for c in range(3):
                xi_ref[c, inner] = xs[c]
            xi_ref[3, inner] = n + C0
            xi_ref[4, inner] = m
        for c, row in enumerate([xs[0] * -2.0, xs[1] * -2.0, xs[2] * -2.0, n]):
            j_ref[pl.ds(c, CELLS, stride=8), :] = row
            j_ref[pl.ds(c + 4, CELLS, stride=8), :] = row
        for c, row in enumerate([xs[0] * m, xs[1] * m, xs[2] * m, m]):
            head = rounded(row)
            w_ref[k, pl.ds(c, CELLS, stride=8), :] = head
            w_ref[k, pl.ds(c + 4, CELLS, stride=8), :] = row - head
        for g in range(CELLS // 16):
            tt_ref[k, g] = j_ref[pl.ds(g * 128, 128), :].T

    zero8 = jnp.zeros((8, TILE), F32)

    def spread(table, base, slot):
        for c in range(4):
            lb_ref[slot, c] = jnp.take_along_axis(table, jnp.full((TILE, TILE), base + c, jnp.int32), axis=1)

    def stage(k, n, slot):
        spread(tt_ref[k, n // 16], lax.rem(n, 16) * 8, slot)

    def pairs(weights, slot, centres):
        weights = jnp.concatenate([weights, zero8], axis=0).astype(BF16)
        ax, ay, az, nj = [lb_ref[slot, c] for c in range(4)]
        for i in centres:
            x, y, z, n = [xi_ref[c, pl.ds(i + 8, 1), :] for c in range(4)]
            u = ((ax * x + ay * y) + (az * z + nj)) + n
            w = jnp.exp2(jnp.log2(u) * -1.5 - u)
            head = w.astype(BF16)
            rest = (w - head.astype(F32)).astype(BF16)
            pull = jnp.dot(weights, head, preferred_element_type=F32) + jnp.dot(weights, rest, preferred_element_type=F32)
            acc_ref[pl.ds(pl.multiple_of((i + 9) * 8, 8), 8), :] += pull[:8]

    def cell(k, n, slot):
        pairs(w_ref[k, pl.ds(pl.multiple_of(n * 8, 8), 8), :], slot, (n - 1, n, n + 1))

    def whole_slab(k, own=False):
        def step(t, carry):
            if own:

                @pl.when(t == turn)
                def _():
                    early[0].start()

            for i in range(UNROLL):
                n = t * UNROLL + i
                stage(k, jnp.minimum(n + 1, CELLS - 1), (i + 1) % UNROLL)
                cell(k, n, i)
            return carry

        stage(k, 0, 0)
        lax.fori_loop(0, CELLS // UNROLL, step, 0)

    prepare(0)
    whole_slab(0, own=True)

    speed = merged(1, 3)
    for c in range(3):
        v_ref[c] = speed[c]
    early.append(remote(v_ref, bv_ref, early_s.at[1], early_r.at[1], (other, p)))
    early[1].start()

    near = jnp.where(lax.rem(s, FAR) == 0, 2, 1)
    far = 3 - near

    def arrived(k):
        remote(x_ref.at[0], x_ref.at[k], halo_s.at[k - 1], halo_r.at[k - 1], (up, p)).wait_recv()

    arrived(near)
    prepare(near)
    whole_slab(near)

    for e, copy in enumerate(edges):
        copy.wait_recv()
        tile = edge_in[e]
        xs = [tile[c : c + 1] * KAP for c in range(3)]
        m = tile[3:4]
        n = xs[0] * xs[0] + xs[1] * xs[1] + xs[2] * xs[2]
        for c, row in enumerate([xs[0] * -2.0, xs[1] * -2.0, xs[2] * -2.0, n]):
            je_ref[e * 8 + c : e * 8 + c + 1] = row
        for c, row in enumerate([xs[0] * m, xs[1] * m, xs[2] * m, m]):
            head = rounded(row)
            we_ref[e * 8 + c : e * 8 + c + 1] = head
            we_ref[e * 8 + c + 4 : e * 8 + c + 5] = row - head
    te_ref[...] = je_ref[...].T
    for e in range(6):
        spread(te_ref[...], e * 8, e)
        pairs(we_ref[e * 8 : e * 8 + 8], e, (0 if e < 3 else CELLS - 1,))

    arrived(far)
    prepare(far)

    def finish(row):
        total = []
        for c in range(4):
            at = pl.multiple_of((row + 1) * 8, 8)
            total.append(acc_ref[pl.ds(at + c, 8, stride=8), :] + acc_ref[pl.ds(at + c + 4, 8, stride=8), :])
        live = xi_ref[4, pl.ds(row, 8)] > 0
        for c in range(3):
            pull = (total[c] - xi_ref[c, pl.ds(row, 8)] * total[3]) * SCALE
            ac_ref[c, pl.ds(row, 8)] = jnp.where(live, pull, 0.0)

    def late(k, rows):
        part = pl.ds(pl.multiple_of(k * 16, 8), rows)
        return remote(ac_ref.at[:, part], ba_ref.at[:, part], late_s.at[k], late_r.at[k], (other, p))

    stage(far, 0, 0)

    def chunk(k, carry):
        def step(t, carry):
            for i in range(UNROLL):
                n = k * 16 + t * UNROLL + i
                stage(far, jnp.minimum(n + 1, CELLS - 1), (i + 1) % UNROLL)
                cell(far, n, i)
            return carry

        lax.fori_loop(0, 16 // UNROLL, step, 0)
        row = pl.multiple_of(k * 16, 8)
        finish(row)
        finish(row + 8)
        late(k, 16).start()
        return carry

    lax.fori_loop(0, CELLS // 16, chunk, 0)
    finish(CELLS)
    last = CELLS // 16
    late(last, 8).start()

    def store(src, dst):
        outs.append(pltpu.make_async_copy(src, dst, out_s.at[len(outs)]))
        outs[-1].start()

    inner = pl.ds(8, CELLS)
    sv_ref[...] = v_ref[...] + kick_step * ac_ref[:, inner]
    store(sv_ref, state_ref.at[4:7])
    store(ac_ref.at[:, inner], state_ref.at[7:10])
    for copy in early:
        copy.wait_recv()
    store(bx_ref, buddy_ref.at[0:4])
    for k in range(last + 1):
        late(k, 16 if k < last else 8).wait_recv()
    store(ba_ref.at[:, inner], buddy_ref.at[7:10])
    bw_ref[...] = bv_ref[...] + kick_step * ba_ref[:, inner]
    store(bw_ref, buddy_ref.at[4:7])
    for copy in outs:
        copy.wait()
    for copy in route[0] + route[1] + halo + edges + early:
        copy.wait_send()
    for k in range(last + 1):
        late(k, 16 if k < last else 8).wait_send()


def written(state_ref, buddy_ref, state_out, buddy_out, sem):
    copies = [
        pltpu.make_async_copy(state_ref, state_out, sem.at[0]),
        pltpu.make_async_copy(buddy_ref, buddy_out, sem.at[1]),
    ]
    for copy in copies:
        copy.start()
    for copy in copies:
        copy.wait()


def per_device(positions, velocities, masses, owner_cell, counts):
    n_slab, n_dom = lax.axis_size("slab"), lax.axis_size("dom")
    rows = positions.shape[1]
    out = jax.ShapeDtypeStruct((10, CELLS, TILE), F32)
    block = (CELLS, TILE)
    dma = pltpu.SemaphoreType.DMA
    state, buddy = pl.pallas_call(
        functools.partial(kernel, n_slab, n_dom),
        out_shape=(out, out),
        in_specs=[pl.BlockSpec(memory_space=pltpu.HBM)] * 4 + [pl.BlockSpec(memory_space=pltpu.SMEM)],
        out_specs=(pl.BlockSpec(memory_space=pl.ANY),) * 2,
        scratch_shapes=[
            pltpu.VMEM((3, rows), F32),
            pltpu.VMEM((3, rows), F32),
            pltpu.VMEM((1, rows), F32),
            pltpu.VMEM((1, rows), jnp.int32),
            pltpu.VMEM((PARTS * 4 * SLOT, GROUP * BLOCK), BF16),
            pltpu.VMEM((PARTS * 3 * SLOT, rows), BF16),
            pltpu.VMEM((256, rows), BF16),
            pltpu.VMEM((PARTS * 4 * SLOT, 256), F32),
            pltpu.VMEM((2, 256, 128), F32),
            pltpu.VMEM((2, 3, *block), F32),
            pltpu.VMEM((3, 4, *block), F32),
            pltpu.VMEM((2, 8, TILE), F32),
            pltpu.VMEM((6, 8, TILE), F32),
            pltpu.VMEM((3, *block), F32),
            pltpu.VMEM((3, CELLS + 8, TILE), F32),
            pltpu.VMEM((4, *block), F32),
            pltpu.VMEM((3, *block), F32),
            pltpu.VMEM((3, CELLS + 8, TILE), F32),
            pltpu.VMEM((3, *block), F32),
            pltpu.VMEM((3, *block), F32),
            pltpu.VMEM((5, CELLS + 16, TILE), F32),
            pltpu.VMEM((CELLS * 8, TILE), F32),
            pltpu.VMEM((3, CELLS * 8, TILE), F32),
            pltpu.VMEM((3, CELLS // 16, TILE, TILE), F32),
            pltpu.VMEM((TILE, TILE), F32),
            pltpu.VMEM((48, TILE), F32),
            pltpu.VMEM((TILE, TILE), F32),
            pltpu.VMEM(((CELLS + 10) * 8, TILE), F32),
            pltpu.VMEM((UNROLL, 4, TILE, TILE), F32),
            dma((2, 3)), dma((2, 3)), dma((2,)), dma((2,)), dma((6,)), dma((6,)), dma((2,)), dma((2,)), dma((5,)), dma((5,)), dma((6,)), dma((4,)),
        ],
        compiler_params=pltpu.CompilerParams(collective_id=0, has_side_effects=True, vmem_limit_bytes=VMEM_LIMIT),
        name="substep",
    )(*[pltpu.with_memory_space_constraint(a, pltpu.HBM) for a in (positions, velocities, masses.reshape(1, -1), owner_cell.reshape(1, -1))], counts)
    here = pl.BlockSpec(memory_space=pl.ANY)
    state, buddy = pl.pallas_call(
        written,
        out_shape=(out, out),
        in_specs=[here] * 2,
        out_specs=(pl.BlockSpec(memory_space=pltpu.HBM),) * 2,
        scratch_shapes=[dma((2,))],
        compiler_params=pltpu.CompilerParams(vmem_limit_bytes=1 << 20),
        name="written",
    )(state, buddy)
    return state[:, None], buddy[:, None]


def solution(mesh):
    placed = (
        P(None, ("slab", "dom")),
        P(None, ("slab", "dom")),
        P(("slab", "dom")),
        P(("slab", "dom"), None),
        P(("slab", "dom")),
    )
    return jax.shard_map(
        per_device,
        mesh=mesh,
        in_specs=placed,
        out_specs=(P(None, "slab", "dom", None), P(None, "slab", "dom", None)),
        check_vma=False,
    )
```

```python
import functools
import math

import jax
import jax.numpy as jnp
from jax import lax
from jax.experimental import pallas as pl
from jax.experimental.pallas import tpu as pltpu
from jax.sharding import PartitionSpec as P

CELLS = 64
TILE = 128
SLOT = 32
BLOCK = 256
GROUP = 8
PARTS = 2
UNROLL = 16
VMEM_LIMIT = 24 << 20
SHARED = 32
FAR = 8
F32, BF16 = jnp.float32, jnp.bfloat16
MESH = pl.DeviceIdType.MESH

drift_step = 0.5
kick_step = 0.5
soften = 0.25
reach = 4.0
coupling = 0.25
KAP = math.sqrt(math.log2(math.e) / reach)
C0 = KAP * KAP * soften
SCALE = coupling * 2.0**C0 * KAP**2


def rounded(x):
    return x.astype(BF16).astype(F32)


def place_rows(pos_ref, vel_ref, mass_ref, own_ref, cnt_ref, a_ref, av_ref, b_ref, d_ref):
    rows = pos_ref.shape[1]
    before = lax.broadcasted_iota(jnp.int32, (BLOCK, BLOCK), 0) < lax.broadcasted_iota(jnp.int32, (BLOCK, BLOCK), 1)
    tri = jnp.concatenate([before.astype(BF16), jnp.ones((BLOCK, 128), BF16)], axis=1)
    owner = lax.broadcasted_iota(jnp.int32, (256, BLOCK), 0)
    ranks = lax.broadcasted_iota(jnp.int32, (SLOT, BLOCK), 0).astype(F32)
    lane = lax.broadcasted_iota(jnp.int32, (1, BLOCK), 1)
    live = cnt_ref[0]
    d_ref[...] = jnp.zeros_like(d_ref)

    def group(g, prefix):
        whole = pl.ds(pl.multiple_of(g * GROUP * BLOCK, BLOCK), GROUP * BLOCK)
        for q in range(GROUP):
            off = pl.multiple_of((g * GROUP + q) * BLOCK, BLOCK)
            rows_here = pl.ds(off, BLOCK)
            hot = owner == jnp.where(lane + off < live, own_ref[:, rows_here], -1)
            hot16 = jnp.where(hot, 1.0, 0.0).astype(BF16)
            b_ref[:, rows_here] = hot16
            seen = jnp.dot(hot16, tri, preferred_element_type=F32)
            earlier = seen[:, :BLOCK] + jnp.concatenate([prefix, prefix], axis=1)
            prefix = prefix + seen[:, BLOCK:]
            rank = ranks == jnp.sum(jnp.where(hot, earlier, 0.0), axis=0, keepdims=True)

            def put(ref, values, where):
                for c, value in enumerate(values):
                    for piece in range(PARTS):
                        head = rounded(value)
                        at = pl.ds((piece * len(values) + c) * SLOT, SLOT)
                        ref[at, where] = jnp.where(rank, head, 0.0).astype(BF16)
                        value = value - head

            v = vel_ref[:, rows_here]
            x = pos_ref[:, rows_here] + drift_step * v
            put(a_ref, [x[0:1], x[1:2], x[2:3], mass_ref[:, rows_here]], pl.ds(q * BLOCK, BLOCK))
            put(av_ref, [v[0:1], v[1:2], v[2:3]], rows_here)
        d_ref[...] += product(a_ref[...], b_ref[:, whole])
        return prefix

    lax.fori_loop(0, rows // (GROUP * BLOCK), group, jnp.zeros((256, 128), F32))


def product(a, b):
    return lax.dot_general(a, b, (((1,), (1,)), ((), ())), preferred_element_type=F32)


def summed(pieces, size):
    total = pieces[0:size]
    for piece in range(1, PARTS):
        total = total + pieces[piece * size : (piece + 1) * size]
    return total


def kernel(
    n_slab, n_dom,
    pos_hbm, vel_hbm, mass_hbm, own_hbm, cnt_ref, state_ref, buddy_ref, pos_ref, vel_ref, mass_ref, own_ref,
    a_ref, av_ref, b_ref, d_ref, sent_ref, got_ref, x_ref, edge_out, edge_in, v_ref, ac_ref, bx_ref, bv_ref, ba_ref,
    sv_ref, bw_ref, sa_ref, sb_ref, ae_ref, re_ref, xi_ref, j_ref, w_ref, tt_ref, je_ref, we_ref, te_ref, acc_ref, lb_ref,
    route_s, route_r, halo_s, halo_r, edge_s, edge_r, early_s, early_r, late_s, late_r, back_s, back_r, out_s, in_s,
):
    s, p = lax.axis_index("slab"), lax.axis_index("dom")
    up, down = lax.rem(s + 1, n_slab), lax.rem(s + n_slab - 1, n_slab)
    right, left = lax.rem(p + 1, n_dom), lax.rem(p + n_dom - 1, n_dom)
    other = lax.rem(s + n_slab // 2, n_slab)
    ahead = s < n_slab // 2

    pairs_in = ((own_hbm, own_ref), (pos_hbm, pos_ref), (vel_hbm, vel_ref), (mass_hbm, mass_ref))
    loads = [pltpu.make_async_copy(src, dst, in_s.at[i]) for i, (src, dst) in enumerate(pairs_in)]
    for copy in loads:
        copy.start()
    barrier = pltpu.get_barrier_semaphore()
    peers = [(s, lax.rem(p + t, n_dom)) for t in range(1, n_dom)]
    peers += [(a, b) for a in (up, down) for b in (p, left, right)]
    peers += [(other, p)]
    for peer in peers:
        pl.semaphore_signal(barrier, inc=1, device_id=peer, device_id_type=MESH)

    acc_ref[...] = jnp.zeros_like(acc_ref)
    xi_ref[...] = jnp.full(xi_ref.shape, C0, F32)
    xi_ref[4] = jnp.zeros(xi_ref.shape[1:], F32)
    edge_out[...] = jnp.zeros_like(edge_out)
    je_ref[...] = jnp.zeros_like(je_ref)
    for copy in loads:
        copy.wait()
    place_rows(pos_ref, vel_ref, mass_ref, own_ref, cnt_ref, a_ref, av_ref, b_ref, d_ref)

    def pack(half, placed):
        for cols in (slice(0, 128), slice(128, 256)):
            sent_ref[half, cols] = pltpu.roll(placed[:, cols].T, p * SLOT, 1)

    pack(0, summed(d_ref[...], 4 * SLOT))
    pl.semaphore_wait(barrier, len(peers))

    def remote(src, dst, send, recv, device):
        return pltpu.make_async_remote_copy(
            src_ref=src, dst_ref=dst, send_sem=send, recv_sem=recv, device_id=device, device_id_type=MESH
        )

    route = [[], []]

    def send_rows(half):
        for t in range(1, n_dom):
            q = lax.rem(p + t, n_dom)
            copy = remote(
                sent_ref.at[half, pl.ds(pl.multiple_of(q * CELLS, CELLS), CELLS)], got_ref.at[half, t - 1],
                route_s.at[half, t - 1], route_r.at[half, t - 1], (s, q),
            )
            copy.start()
            route[half].append(copy)

    send_rows(0)
    speeds = summed(product(av_ref[...], b_ref[...]), 3 * SLOT)
    pack(1, jnp.concatenate([speeds, jnp.zeros((SLOT, 256), F32)], axis=0))
    send_rows(1)
    lane_group = lax.broadcasted_iota(jnp.int32, (CELLS, TILE), 1) // SLOT

    def merged(half, count):
        pieces = [(p, sent_ref[half, pl.ds(pl.multiple_of(p * CELLS, CELLS), CELLS)])]
        for t in range(1, n_dom):
            route[half][t - 1].wait_recv()
            pieces.append((lax.rem(p + n_dom - t, n_dom), got_ref[half, t - 1]))
        out = []
        for c in range(count):
            full = jnp.zeros((CELLS, TILE), F32)
            for source, piece in pieces:
                full = jnp.where(lane_group == lax.rem(source + c, n_dom), piece, full)
            out.append(full if c == 0 else pltpu.roll(full, TILE - c * SLOT, 1))
        return out

    own = merged(0, 4)
    for c in range(4):
        x_ref[0, c] = own[c]
        edge_out[0, c : c + 1] = own[c][0:1]
        edge_out[1, c : c + 1] = own[c][CELLS - 1 : CELLS]
    halo = [
        remote(x_ref.at[0], x_ref.at[k + 1], halo_s.at[k], halo_r.at[k], (to, p)) for k, to in enumerate((up, down))
    ]
    edges = []
    for side, to_dom, source in ((0, right, 1), (1, left, 0)):
        for k, to_slab in enumerate((s, up, down)):
            e = side * 3 + k
            edges.append(remote(edge_out.at[source], edge_in.at[e], edge_s.at[e], edge_r.at[e], (to_slab, to_dom)))
    for copy in halo + edges:
        copy.start()
    outs = [pltpu.make_async_copy(x_ref.at[0], state_ref.at[0:4], out_s.at[0])]
    outs[0].start()
    early = [remote(x_ref.at[0], bx_ref, early_s.at[0], early_r.at[0], (other, p))]
    crossing = lax.rem(s + 2, 2 * FAR) < 4
    turn = jnp.where(crossing, jnp.where(ahead, 2, 1), 0)

    def prepare(k, buddy=False):
        values = [bx_ref[c] if buddy else x_ref[k, c] for c in range(4)]
        xs = [value * KAP for value in values[:3]]
        m = values[3]
        n = xs[0] * xs[0] + xs[1] * xs[1] + xs[2] * xs[2]
        if isinstance(k, int):
            inner = pl.ds(8, CELLS)
            for c in range(3):
                xi_ref[c, inner] = xs[c]
            xi_ref[3, inner] = n + C0
            xi_ref[4, inner] = m
        for c, row in enumerate([xs[0] * -2.0, xs[1] * -2.0, xs[2] * -2.0, n]):
            j_ref[pl.ds(c, CELLS, stride=8), :] = row
            j_ref[pl.ds(c + 4, CELLS, stride=8), :] = row
        for c, row in enumerate([xs[0] * m, xs[1] * m, xs[2] * m, m]):
            head = rounded(row)
            w_ref[k, pl.ds(c, CELLS, stride=8), :] = head
            w_ref[k, pl.ds(c + 4, CELLS, stride=8), :] = row - head
        for g in range(CELLS // 16):
            tt_ref[k, g] = j_ref[pl.ds(g * 128, 128), :].T

    zero8 = jnp.zeros((8, TILE), F32)

    def spread(table, base, slot):
        for c in range(4):
            lb_ref[slot, c] = jnp.take_along_axis(table, jnp.full((TILE, TILE), base + c, jnp.int32), axis=1)

    def stage(k, n, slot):
        spread(tt_ref[k, n // 16], lax.rem(n, 16) * 8, slot)

    def pairs(weights, slot, centres):
        weights = jnp.concatenate([weights, zero8], axis=0).astype(BF16)
        ax, ay, az, nj = [lb_ref[slot, c] for c in range(4)]
        for i in centres:
            x, y, z, n = [xi_ref[c, pl.ds(i + 8, 1), :] for c in range(4)]
            u = ((ax * x + ay * y) + (az * z + nj)) + n
            w = jnp.exp2(jnp.log2(u) * -1.5 - u)
            head = w.astype(BF16)
            rest = (w - head.astype(F32)).astype(BF16)
            pull = jnp.dot(weights, head, preferred_element_type=F32) + jnp.dot(weights, rest, preferred_element_type=F32)
            acc_ref[pl.ds(pl.multiple_of((i + 9) * 8, 8), 8), :] += pull[:8]

    def cell(k, n, slot):
        pairs(w_ref[k, pl.ds(pl.multiple_of(n * 8, 8), 8), :], slot, (n - 1, n, n + 1))

    def whole_slab(k, own=False):
        def step(t, carry):
            if own:

                @pl.when(t == turn)
                def _():
                    early[0].start()

            for i in range(UNROLL):
                n = t * UNROLL + i
                stage(k, jnp.minimum(n + 1, CELLS - 1), (i + 1) % UNROLL)
                cell(k, n, i)
            return carry

        stage(k, 0, 0)
        cells = jnp.where(ahead, CELLS, CELLS - SHARED) if own else CELLS
        lax.fori_loop(0, cells // UNROLL, step, 0)

    prepare(0)
    whole_slab(0, own=True)

    speed = merged(1, 3)
    for c in range(3):
        v_ref[c] = speed[c]
    early.append(remote(v_ref, bv_ref, early_s.at[1], early_r.at[1], (other, p)))
    early[1].start()

    near = jnp.where(lax.rem(s, FAR) == 0, 2, 1)
    far = 3 - near

    def arrived(k):
        remote(x_ref.at[0], x_ref.at[k], halo_s.at[k - 1], halo_r.at[k - 1], (up, p)).wait_recv()

    arrived(near)
    prepare(near)
    whole_slab(near)

    for e, copy in enumerate(edges):
        copy.wait_recv()
        tile = edge_in[e]
        xs = [tile[c : c + 1] * KAP for c in range(3)]
        m = tile[3:4]
        n = xs[0] * xs[0] + xs[1] * xs[1] + xs[2] * xs[2]
        for c, row in enumerate([xs[0] * -2.0, xs[1] * -2.0, xs[2] * -2.0, n]):
            je_ref[e * 8 + c : e * 8 + c + 1] = row
        for c, row in enumerate([xs[0] * m, xs[1] * m, xs[2] * m, m]):
            head = rounded(row)
            we_ref[e * 8 + c : e * 8 + c + 1] = head
            we_ref[e * 8 + c + 4 : e * 8 + c + 5] = row - head
    te_ref[...] = je_ref[...].T
    for e in range(6):
        spread(te_ref[...], e * 8, e)
        pairs(we_ref[e * 8 : e * 8 + 8], e, (0 if e < 3 else CELLS - 1,))

    arrived(far)
    prepare(far)

    def finish(row, to):
        total = []
        for c in range(4):
            at = pl.multiple_of((row + 1) * 8, 8)
            total.append(acc_ref[pl.ds(at + c, 8, stride=8), :] + acc_ref[pl.ds(at + c + 4, 8, stride=8), :])
        live = xi_ref[4, pl.ds(row, 8)] > 0
        for c in range(3):
            pull = (total[c] - xi_ref[c, pl.ds(row, 8)] * total[3]) * SCALE
            to[c, pl.ds(row, 8)] = jnp.where(live, pull, 0.0)

    def late(k, rows):
        part = pl.ds(pl.multiple_of(k * 16, 8), rows)
        return remote(ac_ref.at[:, part], ba_ref.at[:, part], late_s.at[k], late_r.at[k], (other, p))

    stage(far, 0, 0)

    def chunk(k, carry):
        def step(t, carry):
            for i in range(UNROLL):
                n = k * 16 + t * UNROLL + i
                stage(far, jnp.minimum(n + 1, CELLS - 1), (i + 1) % UNROLL)
                cell(far, n, i)
            return carry

        lax.fori_loop(0, 16 // UNROLL, step, 0)
        row = pl.multiple_of(k * 16, 8)
        finish(row, ac_ref)
        finish(row + 8, ac_ref)
        late(k, 16).start()
        return carry

    lax.fori_loop(0, CELLS // 16, chunk, 0)
    finish(CELLS, ac_ref)
    last = CELLS // 16
    late(last, 8).start()

    def store(src, dst):
        outs.append(pltpu.make_async_copy(src, dst, out_s.at[len(outs)]))
        outs[-1].start()

    early[0].wait_recv()
    store(bx_ref, buddy_ref.at[0:4])

    def back(k):
        part = (pl.ds(SHARED, 16), pl.ds(SHARED + 16, 24))[k]
        return remote(ae_ref.at[:, part], re_ref.at[:, part], back_s.at[k], back_r.at[k], (other, p))

    @pl.when(ahead)
    def _():
        prepare(0, buddy=True)
        acc_ref[...] = jnp.zeros_like(acc_ref)
        stage(0, CELLS - SHARED, 0)
        for k in range(2):

            def step(t, carry, k=k):
                for i in range(UNROLL):
                    n = CELLS - SHARED + (k + t) * UNROLL + i
                    stage(0, jnp.minimum(n + 1, CELLS - 1), (i + 1) % UNROLL)
                    cell(0, n, i)
                return carry

            lax.fori_loop(0, 1, step, 0)
            for row in ((32, 40), (48, 56, 64))[k]:
                finish(row, ae_ref)
            back(k).start()

    inner = pl.ds(8, CELLS)
    shared = pl.ds(SHARED, 40)
    sa_ref[...] = ac_ref[:, inner]

    @pl.when(jnp.logical_not(ahead))
    def _():
        for k in range(2):
            back(k).wait_recv()
        sa_ref[:, 24:] += re_ref[:, shared]

    sv_ref[...] = v_ref[...] + kick_step * sa_ref[...]
    store(sv_ref, state_ref.at[4:7])
    store(sa_ref, state_ref.at[7:10])
    early[1].wait_recv()
    for k in range(last + 1):
        late(k, 16 if k < last else 8).wait_recv()
    sb_ref[...] = ba_ref[:, inner]

    @pl.when(ahead)
    def _():
        sb_ref[:, 24:] += ae_ref[:, shared]

    store(sb_ref, buddy_ref.at[7:10])
    bw_ref[...] = bv_ref[...] + kick_step * sb_ref[...]
    store(bw_ref, buddy_ref.at[4:7])
    for copy in outs:
        copy.wait()
    for copy in route[0] + route[1] + halo + edges + early:
        copy.wait_send()
    for k in range(last + 1):
        late(k, 16 if k < last else 8).wait_send()

    @pl.when(ahead)
    def _():
        for k in range(2):
            back(k).wait_send()


def written(state_ref, buddy_ref, state_out, buddy_out, sem):
    copies = [
        pltpu.make_async_copy(state_ref, state_out, sem.at[0]),
        pltpu.make_async_copy(buddy_ref, buddy_out, sem.at[1]),
    ]
    for copy in copies:
        copy.start()
    for copy in copies:
        copy.wait()


def per_device(positions, velocities, masses, owner_cell, counts):
    n_slab, n_dom = lax.axis_size("slab"), lax.axis_size("dom")
    rows = positions.shape[1]
    out = jax.ShapeDtypeStruct((10, CELLS, TILE), F32)
    block = (CELLS, TILE)
    dma = pltpu.SemaphoreType.DMA
    state, buddy = pl.pallas_call(
        functools.partial(kernel, n_slab, n_dom),
        out_shape=(out, out),
        in_specs=[pl.BlockSpec(memory_space=pltpu.HBM)] * 4 + [pl.BlockSpec(memory_space=pltpu.SMEM)],
        out_specs=(pl.BlockSpec(memory_space=pl.ANY),) * 2,
        scratch_shapes=[
            pltpu.VMEM((3, rows), F32),
            pltpu.VMEM((3, rows), F32),
            pltpu.VMEM((1, rows), F32),
            pltpu.VMEM((1, rows), jnp.int32),
            pltpu.VMEM((PARTS * 4 * SLOT, GROUP * BLOCK), BF16),
            pltpu.VMEM((PARTS * 3 * SLOT, rows), BF16),
            pltpu.VMEM((256, rows), BF16),
            pltpu.VMEM((PARTS * 4 * SLOT, 256), F32),
            pltpu.VMEM((2, 256, 128), F32),
            pltpu.VMEM((2, 3, *block), F32),
            pltpu.VMEM((3, 4, *block), F32),
            pltpu.VMEM((2, 8, TILE), F32),
            pltpu.VMEM((6, 8, TILE), F32),
            pltpu.VMEM((3, *block), F32),
            pltpu.VMEM((3, CELLS + 8, TILE), F32),
            pltpu.VMEM((4, *block), F32),
            pltpu.VMEM((3, *block), F32),
            pltpu.VMEM((3, CELLS + 8, TILE), F32),
            pltpu.VMEM((3, *block), F32),
            pltpu.VMEM((3, *block), F32),
            pltpu.VMEM((3, *block), F32),
            pltpu.VMEM((3, *block), F32),
            pltpu.VMEM((3, CELLS + 8, TILE), F32),
            pltpu.VMEM((3, CELLS + 8, TILE), F32),
            pltpu.VMEM((5, CELLS + 16, TILE), F32),
            pltpu.VMEM((CELLS * 8, TILE), F32),
            pltpu.VMEM((3, CELLS * 8, TILE), F32),
            pltpu.VMEM((3, CELLS // 16, TILE, TILE), F32),
            pltpu.VMEM((TILE, TILE), F32),
            pltpu.VMEM((48, TILE), F32),
            pltpu.VMEM((TILE, TILE), F32),
            pltpu.VMEM(((CELLS + 10) * 8, TILE), F32),
            pltpu.VMEM((UNROLL, 4, TILE, TILE), F32),
            dma((2, 3)), dma((2, 3)), dma((2,)), dma((2,)), dma((6,)), dma((6,)), dma((2,)), dma((2,)), dma((5,)), dma((5,)), dma((2,)), dma((2,)), dma((6,)), dma((4,)),
        ],
        compiler_params=pltpu.CompilerParams(collective_id=0, has_side_effects=True, vmem_limit_bytes=VMEM_LIMIT),
        name="substep",
    )(*[pltpu.with_memory_space_constraint(a, pltpu.HBM) for a in (positions, velocities, masses.reshape(1, -1), owner_cell.reshape(1, -1))], counts)
    here = pl.BlockSpec(memory_space=pl.ANY)
    state, buddy = pl.pallas_call(
        written,
        out_shape=(out, out),
        in_specs=[here] * 2,
        out_specs=(pl.BlockSpec(memory_space=pltpu.HBM),) * 2,
        scratch_shapes=[dma((2,))],
        compiler_params=pltpu.CompilerParams(vmem_limit_bytes=1 << 20),
        name="written",
    )(state, buddy)
    return state[:, None], buddy[:, None]


def solution(mesh):
    placed = (
        P(None, ("slab", "dom")),
        P(None, ("slab", "dom")),
        P(("slab", "dom")),
        P(("slab", "dom"), None),
        P(("slab", "dom")),
    )
    return jax.shard_map(
        per_device,
        mesh=mesh,
        in_specs=placed,
        out_specs=(P(None, "slab", "dom", None), P(None, "slab", "dom", None)),
        check_vma=False,
    )
```
